32 devices in a mesh: row: 4 (over y, x), col: 8 (over z, core).
Axes of the slice: x: 2, y: 2, z: 4, core: 2. Of those that a mesh axis runs over, the one named last changes fastest.
Arguments:
- stiffness: float32 [12, 4, 128, 6144], P(None, 'row', None, 'col'), may hold values from -8 to 8
- lower_first: float32 [1024, 10, 4, 128], P('col', None, 'row'), may hold values from -0.1875 to 0.1875
- lower_second: float32 [1024, 8, 4, 128], P('col', None, 'row'), may hold values from -0.1875 to 0.1875
- diag_inv: float32 [2, 1024, 2, 4, 128], P(None, 'col', None, 'row'), as said below
Outputs:
- reduced: float32 [12, 4, 128, 6144], P(None, 'row', None, 'col')
The draws below stay inside these ranges and needn't reach their ends.
Inputs may be any that keep to these rules, and one draw needn't show every extreme that they name: Each block of diag_inv, read as a 1024 x 1024 matrix, is zero above its diagonal and has a positive diagonal.
All inputs are finite; a program needn't handle non-finite values.
Results may differ from the reference program's by a relative error of at most 0.000086.
Values sent between devices are 32-bit elements; how exact they have to be, the bound alone decides.
A program may use at most 128 MiB of HBM per device.

```python
import jax
import jax.numpy as jnp
from jax import lax

NB = 1024
RBLK = 128
CYCLES = 12
PC = 2
LCYC = 10
ROWS = 6144
COLS = 6144
N_ROW = 4


def draw_diag_inv(key, part):
    key_off, key_diag = jax.random.split(jax.random.fold_in(key, 7))
    row_idx = jnp.arange(NB, dtype=jnp.int32)[:, None]
    col_idx = jnp.arange(NB, dtype=jnp.int32)[None, :]
    offdiag = jax.random.normal(key_off, (2, NB, NB), jnp.float32)
    diagonal = jnp.exp(jax.random.uniform(key_diag, (2, NB, NB), jnp.float32, -0.69, 0.69))
    scaled = offdiag / jnp.sqrt(jnp.float32(NB))
    matrix = jnp.where(col_idx < row_idx, scaled, jnp.where(col_idx == row_idx, diagonal, 0.0))
    return matrix.astype(jnp.float32).reshape(2, NB, PC, N_ROW, RBLK)


def level_of(stream_key, shape, cuts, least, largest):
    def one(dim, shards_of):
        steps = jax.random.uniform(jax.random.fold_in(jax.random.fold_in(stream_key, 6), dim), (shards_of,), jnp.float32, least / len(cuts), largest / len(cuts))
        return jnp.repeat(jnp.exp(steps), shape[dim] // shards_of).reshape((-1,) + (1,) * (len(shape) - dim - 1))

    level = one(*cuts[0])
    for cut in cuts[1:]:
        level = level * one(*cut)
    return level


def noise(own_key, shape, deviation, most, shards=(), held_as=jnp.bfloat16):
    entries = jax.random.normal(own_key, shape, jnp.float32) * deviation
    if len(shards) > 0:
        entries = level_of(own_key, shape, shards, -0.22, 0.18) * entries
    return jnp.clip(entries, min=-most, max=most).astype(held_as)


def setup_inputs(seed: int = 0) -> dict:
    seeds = jax.random.split(jax.random.key(seed), 5)
    stiffness = noise(seeds[0], (CYCLES, N_ROW, RBLK, COLS), 1.0, 8.0, ((1, 4), (3, 8)), jnp.float32)
    lower_first = noise(seeds[1], (NB, LCYC, N_ROW, RBLK), NB ** -0.5, 0.1875, ((0, 8), (2, 4)), jnp.float32)
    lower_second = noise(seeds[2], (NB, LCYC - PC, N_ROW, RBLK), NB ** -0.5, 0.1875, ((0, 8), (2, 4)), jnp.float32)
    diag_inv = draw_diag_inv(jax.random.fold_in(seeds[4], 71), 0)
    return dict(stiffness=stiffness, lower_first=lower_first, lower_second=lower_second, diag_inv=diag_inv)


def product(left, right):
    return jnp.dot(left, right, precision=lax.Precision.HIGHEST, preferred_element_type=jnp.float32)


def reference(stiffness, lower_first, lower_second, diag_inv):
    whole = stiffness.reshape(ROWS, COLS)
    inverse = diag_inv.reshape(2, NB, NB)
    first = lower_first.reshape(NB, ROWS - NB)
    second = lower_second.reshape(NB, ROWS - 2 * NB)
    w_first = product(inverse[0], whole[:NB])
    updated = whole[NB:] - product(first.T, w_first)
    w_second = product(inverse[1], updated[:NB])
    remain = updated[NB:] - product(second.T, w_second)
    return jnp.concatenate([w_first, w_second, remain], axis=0).reshape(CYCLES, N_ROW, RBLK, COLS)
```

```python
import jax
import jax.numpy as jnp
from jax import lax
from jax.sharding import PartitionSpec as P


def product(left, right):
    return jnp.dot(left, right, precision=lax.Precision.HIGH, preferred_element_type=jnp.float32)


def apply_cols(columns, factor):
    return lax.dot_general(
        columns,
        factor,
        (((0,), (0,)), ((), ())),
        precision=lax.Precision.HIGH,
        preferred_element_type=jnp.float32,
    )


def shards(stiffness, lower_first, lower_second, diag_inv):
    cycles = stiffness.shape[0]
    rblk = stiffness.shape[2]
    cdev = stiffness.shape[3]
    pcount = diag_inv.shape[2]
    nrow = lax.axis_size("row")
    nb = diag_inv.shape[1] * lax.axis_size("col")
    height = pcount * rblk
    matrix_rows = stiffness.reshape(cycles * rblk, cdev)
    inv_cols = lax.all_gather(diag_inv, "col", axis=1, tiled=True)
    inverse = inv_cols.reshape(2, nb, height)

    def own_rows(solved):
        grouped = solved.reshape(pcount, nrow, rblk, cdev)
        mine = lax.dynamic_slice_in_dim(grouped, lax.axis_index("row"), 1, 1)
        return mine.reshape(height, cdev)

    w_first = lax.psum(product(inverse[0], matrix_rows[:height]), "row")
    coupling = lax.all_gather(lower_first[:, :pcount], "col", axis=0, tiled=True).reshape(
        nb, height
    )
    w_second = lax.psum(
        product(inverse[1], matrix_rows[height : 2 * height] - apply_cols(coupling, w_first)), "row"
    )
    pieces = (
        lax.all_gather(lower_first[:, pcount:], "col", axis=0, tiled=True),
        lax.all_gather(lower_second, "col", axis=0, tiled=True),
    )
    count = pieces[0].shape[0]
    first_piece = pieces[0].reshape(count, -1)
    second_piece = pieces[1].reshape(count, -1)
    remain = (
        matrix_rows[2 * height :]
        - apply_cols(first_piece, w_first)
        - apply_cols(second_piece, w_second)
    )
    stacked = jnp.concatenate([own_rows(w_first), own_rows(w_second), remain], axis=0)
    return stacked.reshape(cycles, 1, rblk, cdev)


def solution(mesh):
    placed = (
        P(None, "row", None, "col"),
        P("col", None, "row", None),
        P("col", None, "row", None),
        P(None, "col", None, "row", None),
    )
    return jax.shard_map(
        shards, mesh=mesh, in_specs=placed, out_specs=P(None, "row", None, "col"), check_vma=False
    )
```

```python
import functools

import jax
import jax.numpy as jnp
from jax import lax
from jax.experimental import pallas as pl
from jax.experimental.pallas import tpu as pltpu
from jax.sharding import PartitionSpec as P

MESH = pl.DeviceIdType.MESH
F32 = jnp.float32
BF16 = jnp.bfloat16


def split(value):
    high = value.astype(BF16)
    return high, (value - high.astype(F32)).astype(BF16)


def dot3(ah, al, bh, bl):
    d = functools.partial(jnp.dot, preferred_element_type=F32)
    return d(ah, bh) + (d(ah, bl) + d(al, bh))


def kernel(
    dims, k_ref, f_ref, s_ref, d_ref, out_ref,
    kg, ug, fg, sg, dg, kloc, bh, bl, dh, dl, wh, wl, wf, sems, osem,
):
    nrow, ncol, pc, rblk, kb, sem_count = dims
    nchip = ncol // 2
    nb = kb * ncol
    width = k_ref.shape[2]
    cycles = k_ref.shape[0]
    height = pc * rblk
    half_ring = nrow // 2
    row, col = lax.axis_index("row"), lax.axis_index("col")
    q, core = col // 2, col % 2
    partner = col + 1 - 2 * core

    def flip(i):
        return i + (i // half_ring) * (3 * half_ring - 1 - 2 * i)

    pos = flip(row)

    def row_at(shift):
        return flip((pos + shift + nrow) % nrow)

    table = {}

    def sem(*key):
        index = table.setdefault(key, len(table))
        assert index < sem_count
        return sems.at[index]

    sent = []

    def always(fn):
        fn()

    def guard(cond):
        return always if cond is None else pl.when(cond)

    def both(a, b):
        if a is None:
            return b
        return a if b is None else jnp.logical_and(a, b)

    def push(src, dst, skey, rkey, device, cond=None):
        copy = pltpu.make_async_remote_copy(
            src_ref=src, dst_ref=dst, send_sem=sem("s", *skey), recv_sem=sem("r", *rkey),
            device_id=device, device_id_type=MESH,
        )
        guard(cond)(copy.start)
        sent.append((cond, copy))

    def arrived(dst, rkey, device):
        pltpu.make_async_remote_copy(
            src_ref=dst, dst_ref=dst, send_sem=sem("s", *rkey), recv_sem=sem("r", *rkey),
            device_id=device, device_id_type=MESH,
        ).wait_recv()

    barrier = pltpu.get_barrier_semaphore()
    right, left = {"row": row_at(1)}, {"row": row_at(-1)}
    up, down, mate = {"col": col + 2}, {"col": col - 2}, {"col": partner}
    for device in (right, left, mate):
        pl.semaphore_signal(barrier, inc=1, device_id=device, device_id_type=MESH)
    has_up, has_down = q < nchip - 1, q > 0

    @pl.when(has_up)
    def _():
        pl.semaphore_signal(barrier, inc=1, device_id=up, device_id_type=MESH)

    @pl.when(has_down)
    def _():
        pl.semaphore_signal(barrier, inc=1, device_id=down, device_id_type=MESH)

    spans = nchip - 1
    pl.semaphore_wait(barrier, 3 + (2 * spans - 1 - q) // spans + (q + spans - 1) // spans)

    def fslot(lo, hi):
        return lambda chip, e: fg.at[pl.ds(pl.multiple_of((chip * 2 + e) * kb, kb), kb), lo:hi]

    def sslot(chip, e):
        return sg.at[pl.ds(pl.multiple_of((chip * 2 + e) * kb, kb), kb), :]

    def dslot(m, p):
        return lambda chip, e: dg.at[m, p, row, chip, e]

    low = [p * nchip // pc for p in range(pc)]
    chains = {}
    for m in range(2):
        for p in range(pc):
            chains["d", m, p] = (low[p], d_ref.at[m, p], dslot(m, p))
    chains["f1"] = (0, f_ref.at[:, :height], fslot(0, height))
    chains["f2"] = (0, f_ref.at[:, height:], fslot(height, f_ref.shape[1]))
    chains["s"] = (0, s_ref, sslot)

    def chain_own(name):
        first, src, slot = chains[name]
        mine = None if first == 0 else q >= first
        local = pltpu.make_async_copy(src, slot(q, core), sem("l", name))
        local.start()
        dst = slot(q, core)
        push(src, dst, (name, "u", 0), (name, "u", 1), up, both(mine, has_up))
        push(src, dst, (name, "d", 0), (name, "d", 1), down, both(mine, has_down))
        push(src, dst, (name, "m", 0), (name, "m", 0), mate, mine)
        return local

    def chain_hop(name, t):
        first, _, slot = chains[name]
        for way, source, more, nxt in (
            ("u", q - t, has_up, up), ("d", q + t, has_down, down)
        ):
            real = source >= first if way == "u" else source < nchip
            if way == "d" and first > 0:
                real = jnp.logical_and(real, source >= first)
            ref = slot(source, core)
            guard(real)(functools.partial(arrived, ref, (name, way, t), nxt))
            if t < nchip - 1:
                push(ref, ref, (name, way, t), (name, way, t + 1), nxt, both(real, more))
            push(ref, ref, (name, "m", way, t), (name, "m", way, t), mate, real)

    def chain_mate(name):
        first, _, slot = chains[name]
        other = 1 - core
        mine = None if first == 0 else q >= first
        guard(mine)(functools.partial(arrived, slot(q, other), (name, "m", 0), mate))
        for t in range(1, nchip):
            for way, source in (("u", q - t), ("d", q + t)):
                real = source >= first if way == "u" else source < nchip
                if way == "d" and first > 0:
                    real = jnp.logical_and(real, source >= first)
                guard(real)(
                    functools.partial(arrived, slot(source, other), (name, "m", way, t), mate)
                )

    def stack(buf):
        def place(origin, part, e):
            if part is None:
                return buf.at[:, origin]
            return buf.at[:, origin, pl.ds(part * (rblk // 2), rblk // 2), :]
        return place

    def dstack(m, p):
        def place(origin, part, e):
            if part is None:
                return dg.at[m, p, origin, low[p]:, e]
            return dg.at[m, p, origin, low[p]:, e, pl.ds(part * (kb // 2), kb // 2), :]
        return place

    rings = {"k": (stack(kg), False), "u": (stack(ug), False)}
    for m in range(2):
        for p in range(pc):
            rings["e", m, p] = (dstack(m, p), True)

    def ring_own(name, src=None):
        place, _ = rings[name]
        own = place(row, None, core)
        src = own if src is None else src
        push(src, own, (name, "R", 0), (name, "R", 1), right)
        push(src, own, (name, "L", 0), (name, "L", 1), left)

    def ring_hop(name, t):
        place, shared = rings[name]
        for way, sign, part, nxt in (("R", -1, 0, right), ("L", 1, 1, left)):
            origin = row_at(sign * t)
            got = None if t < half_ring else part
            ref = place(origin, got, core)
            arrived(ref, (name, way, t), nxt)
            if t < half_ring:
                fwd = place(origin, None if t + 1 < half_ring else part, core)
                push(fwd, fwd, (name, way, t), (name, way, t + 1), nxt)
            if shared:
                push(ref, ref, (name, "m", way, t), (name, "m", way, t), mate)

    def ring_mate(name):
        place, _ = rings[name]
        for t in range(1, half_ring + 1):
            for way, sign, part in (("R", -1, 0), ("L", 1, 1)):
                got = None if t < half_ring else part
                arrived(place(row_at(sign * t), got, 1 - core), (name, "m", way, t), mate)

    hops = range(1, nchip)
    rhops = range(1, half_ring + 1)
    dnames = [[("d", m, p) for p in range(pc)] for m in range(2)]
    enames = [[("e", m, p) for p in range(pc)] for m in range(2)]

    locals_ = {}
    for name in dnames[0] + ["f1"] + dnames[1]:
        locals_[name] = chain_own(name)
    ring_own("k", k_ref.at[:pc])
    kmine = pltpu.make_async_copy(k_ref.at[:pc], kg.at[:, row], sem("l", "k"))
    kmine.start()
    kall = pltpu.make_async_copy(k_ref.at[pc:], kloc, sem("l", "kall"))
    kall.start()
    for t in hops:
        for name in dnames[0]:
            chain_hop(name, t)
    for name, ring in zip(dnames[0], enames[0]):
        locals_[name].wait()
        ring_own(ring)
    for t in hops:
        chain_hop("f1", t)
    for t in hops:
        for name in dnames[1]:
            chain_hop(name, t)
    for name, ring in zip(dnames[1], enames[1]):
        locals_[name].wait()
    locals_["f2"] = chain_own("f2")
    locals_["s"] = chain_own("s")
    for t in rhops:
        ring_hop("k", t)
    for t in rhops:
        for ring in enames[0]:
            ring_hop(ring, t)
    for ring in enames[1]:
        ring_own(ring)
    for name in dnames[0]:
        chain_mate(name)
    for ring in enames[0]:
        ring_mate(ring)
    kmine.wait()

    group = nb // pc
    chunk = 256

    def solve(m, rhs, wbase):
        for p in range(pc):
            for r in range(nrow):
                at = (p * nrow + r) * rblk
                hi, lo = split(rhs[p, r])
                bh[at : at + rblk, :] = hi
                bl[at : at + rblk, :] = lo
                hi, lo = split(dg[m, p, r, low[p]:].reshape(nb - p * group, rblk))
                dh[p * group :, at : at + rblk] = hi
                dl[p * group :, at : at + rblk] = lo
        for g in range(pc):
            rows = slice(g * group, (g + 1) * group)
            deep = (g + 1) * group
            for n in range(0, width, chunk):
                cols = slice(n, n + chunk)
                w = dot3(dh[rows, :deep], dl[rows, :deep], bh[:deep, cols], bl[:deep, cols])
                wf[m, rows, cols] = w
                hi, lo = split(w)
                wh[m, rows, cols] = hi
                wl[m, rows, cols] = lo

    def apply(panel, lo, size, m):
        th, tl = split(panel[:, pl.ds(lo, size)].T)
        return dot3(th, tl, wh[m], wl[m])

    outs = []

    solve(0, kg, 0)
    chain_hop("f2", 1)
    locals_["f1"].wait()
    chain_mate("f1")
    kall.wait()
    first = apply(fg, 0, height, 0)
    ug[:, row] = kloc[:pc] - first.reshape(pc, rblk, width)
    ring_own("u")
    for p in range(pc):
        at = pl.multiple_of((p * nrow + row) * rblk, rblk)
        copy = pltpu.make_async_copy(wf.at[0, pl.ds(at, rblk), :], out_ref.at[p], osem.at[p])
        copy.start()
        outs.append(copy)
    for t in rhops:
        for ring in enames[1]:
            ring_hop(ring, t)
    chain_hop("s", 1)
    if nchip > 2:
        chain_hop("f2", 2)
    ring_hop("u", 1)
    if nchip > 2:
        chain_hop("s", 2)
    for t in rhops[1:]:
        ring_hop("u", t)
    for name in dnames[1]:
        chain_mate(name)
    for ring in enames[1]:
        ring_mate(ring)
    solve(1, ug, 0)
    for p in range(pc):
        at = pl.multiple_of((p * nrow + row) * rblk, rblk)
        copy = pltpu.make_async_copy(wf.at[1, pl.ds(at, rblk), :], out_ref.at[pc + p], osem.at[pc + p])
        copy.start()
        outs.append(copy)
    for t in range(3, nchip):
        chain_hop("f2", t)
    locals_["f2"].wait()
    chain_mate("f2")
    rest = cycles - 2 * pc
    tile = 2 if rest % 2 == 0 else 1
    size = tile * rblk

    def first_tile(i, carry):
        part = apply(fg, pl.multiple_of(height + i * size, rblk), size, 0)
        kloc[pl.ds(pc + i * tile, tile)] -= part.reshape(tile, rblk, width)
        return carry

    lax.fori_loop(0, rest // tile, first_tile, 0)
    for t in range(3, nchip):
        chain_hop("s", t)
    locals_["s"].wait()
    chain_mate("s")

    def second_tile(i, carry):
        part = apply(sg, pl.multiple_of(i * size, rblk), size, 1)
        kloc[pl.ds(pc + i * tile, tile)] -= part.reshape(tile, rblk, width)
        return carry

    lax.fori_loop(0, rest // tile, second_tile, 0)
    last = pltpu.make_async_copy(kloc.at[pc:], out_ref.at[2 * pc :], osem.at[2 * pc])
    last.start()
    outs.append(last)
    for cond, copy in sent:
        guard(cond)(copy.wait_send)
    for copy in outs:
        copy.wait()


def shards(stiffness, lower_first, lower_second, diag_inv):
    cycles, _, rblk, width = stiffness.shape
    nrow, ncol = lax.axis_size("row"), lax.axis_size("col")
    kb = lower_first.shape[0]
    pc = diag_inv.shape[2]
    nb = kb * ncol
    nchip = ncol // 2
    sem_count = (3 + 2 * pc) * (8 * nchip + 8) + 40 * (2 + 2 * pc) * max(1, nrow // 4)
    sem_count = 2 * sem_count
    dims = (nrow, ncol, pc, rblk, kb, sem_count)
    blocks = jnp.transpose(diag_inv[:, :, :, 0, :], (0, 2, 1, 3))
    out = pl.pallas_call(
        functools.partial(kernel, dims),
        out_shape=jax.ShapeDtypeStruct((cycles, rblk, width), F32),
        in_specs=[pl.BlockSpec(memory_space=pl.ANY)] * 4,
        out_specs=pl.BlockSpec(memory_space=pl.ANY),
        scratch_shapes=[
            pltpu.VMEM((pc, nrow, rblk, width), F32),
            pltpu.VMEM((pc, nrow, rblk, width), F32),
            pltpu.VMEM((nb, lower_first.shape[1] * rblk), F32),
            pltpu.VMEM((nb, lower_second.shape[1] * rblk), F32),
            pltpu.VMEM((2, pc, nrow, nchip, 2, kb, rblk), F32),
            pltpu.VMEM((cycles - pc, rblk, width), F32),
            pltpu.VMEM((nb, width), BF16),
            pltpu.VMEM((nb, width), BF16),
            pltpu.VMEM((nb, nb), BF16),
            pltpu.VMEM((nb, nb), BF16),
            pltpu.VMEM((2, nb, width), BF16),
            pltpu.VMEM((2, nb, width), BF16),
            pltpu.VMEM((2, nb, width), F32),
            pltpu.SemaphoreType.DMA((sem_count,)),
            pltpu.SemaphoreType.DMA((2 * pc + 1,)),
        ],
        compiler_params=pltpu.CompilerParams(
            collective_id=0, has_side_effects=True, vmem_limit_bytes=63 << 20
        ),
    )(
        stiffness.reshape(cycles, rblk, width),
        lower_first.reshape(kb, -1),
        lower_second.reshape(kb, -1),
        blocks,
    )
    return out.reshape(cycles, 1, rblk, width)


def solution(mesh):
    placed = (
        P(None, "row", None, "col"),
        P("col", None, "row", None),
        P("col", None, "row", None),
        P(None, "col", None, "row", None),
    )
    return jax.shard_map(
        shards, mesh=mesh, in_specs=placed, out_specs=P(None, "row", None, "col"), check_vma=False
    )
```

```python
import functools

import jax
import jax.numpy as jnp
from jax import lax
from jax.experimental import pallas as pl
from jax.experimental.pallas import tpu as pltpu
from jax.sharding import PartitionSpec as P

MESH = pl.DeviceIdType.MESH
F32 = jnp.float32
BF16 = jnp.bfloat16


def split(value):
    high = value.astype(BF16)
    return high, (value - high.astype(F32)).astype(BF16)


def dot3(ah, al, bh, bl):
    d = functools.partial(jnp.dot, preferred_element_type=F32)
    return d(ah, bh) + (d(ah, bl) + d(al, bh))


def kernel(
    dims, k_ref, f_ref, s_ref, d_ref, out_ref,
    kg, ug, fg, sg, dg, kloc, bh, bl, dh, dl, wh, wl, wf, sems, osem,
):
    nrow, ncol, pc, rblk, kb, sem_count = dims
    nchip = ncol // 2
    nb = kb * ncol
    width = k_ref.shape[2]
    cycles = k_ref.shape[0]
    height = pc * rblk
    half_ring = nrow // 2
    row, col = lax.axis_index("row"), lax.axis_index("col")
    q, core = col // 2, col % 2
    partner = col + 1 - 2 * core

    def flip(i):
        return i + (i // half_ring) * (3 * half_ring - 1 - 2 * i)

    pos = flip(row)

    def row_at(shift):
        return flip((pos + shift + nrow) % nrow)

    table = {}

    def sem(*key):
        index = table.setdefault(key, len(table))
        assert index < sem_count
        return sems.at[index]

    sent = []

    def always(fn):
        fn()

    def guard(cond):
        return always if cond is None else pl.when(cond)

    def both(a, b):
        if a is None:
            return b
        return a if b is None else jnp.logical_and(a, b)

    def push(src, dst, skey, rkey, device, cond=None):
        copy = pltpu.make_async_remote_copy(
            src_ref=src, dst_ref=dst, send_sem=sem("s", *skey), recv_sem=sem("r", *rkey),
            device_id=device, device_id_type=MESH,
        )
        guard(cond)(copy.start)
        sent.append((cond, copy))

    def arrived(dst, rkey, device):
        pltpu.make_async_remote_copy(
            src_ref=dst, dst_ref=dst, send_sem=sem("s", *rkey), recv_sem=sem("r", *rkey),
            device_id=device, device_id_type=MESH,
        ).wait_recv()

    barrier = pltpu.get_barrier_semaphore()
    right, left = {"row": row_at(1)}, {"row": row_at(-1)}
    up, down, mate = {"col": col + 2}, {"col": col - 2}, {"col": partner}
    for device in (right, left, mate):
        pl.semaphore_signal(barrier, inc=1, device_id=device, device_id_type=MESH)
    has_up, has_down = q < nchip - 1, q > 0

    @pl.when(has_up)
    def _():
        pl.semaphore_signal(barrier, inc=1, device_id=up, device_id_type=MESH)

    @pl.when(has_down)
    def _():
        pl.semaphore_signal(barrier, inc=1, device_id=down, device_id_type=MESH)

    spans = nchip - 1
    pl.semaphore_wait(barrier, 3 + (2 * spans - 1 - q) // spans + (q + spans - 1) // spans)

    def fslot(buf, lo, hi):
        return lambda chip, e: buf.at[pl.ds(pl.multiple_of((chip * 2 + e) * kb, kb), kb), lo:hi]

    def dslot(m, p):
        return lambda chip, e: dg.at[m, p, row, chip, e]

    low = [p * nchip // pc for p in range(pc)]
    rest = cycles - 2 * pc
    cut = rest // 2 * rblk
    chains = {}
    for m in range(2):
        for p in range(pc):
            chains["d", m, p] = (low[p], dslot(m, p), d_ref, None)
    chains["f1"] = (0, fslot(fg, 0, height), f_ref, (0, pc))
    chains["f2"] = (0, fslot(fg, height, height + rest * rblk), f_ref, (pc, pc + rest))
    chains["s0"] = (0, fslot(sg, 0, cut), s_ref, (0, rest // 2))
    chains["s1"] = (0, fslot(sg, cut, rest * rblk), s_ref, (rest // 2, rest))

    def stage(name):
        _, slot, src, span = chains[name]
        if span is None:
            _, m, p = name
            pieces = [(src.at[m, :, p, 0, :], slot(q, core))]
        else:
            mine = slot(q, core)
            pieces = [
                (src.at[:, j, 0, :], mine.at[:, (j - span[0]) * rblk : (j - span[0] + 1) * rblk])
                for j in range(*span)
            ]
        copies = []
        for i, (here, there) in enumerate(pieces):
            copies.append(pltpu.make_async_copy(here, there, sem("l", name, i)))
            copies[-1].start()
        return copies

    def chain_own(name, copies):
        first, slot, _, _ = chains[name]
        for copy in copies:
            copy.wait()
        mine = None if first == 0 else q >= first
        own = slot(q, core)
        push(own, own, (name, "u", 0), (name, "u", 1), up, both(mine, has_up))
        push(own, own, (name, "d", 0), (name, "d", 1), down, both(mine, has_down))
        push(own, own, (name, "m", 0), (name, "m", 0), mate, mine)

    def chain_hop(name, t):
        first, slot, _, _ = chains[name]
        for way, source, more, nxt in (
            ("u", q - t, has_up, up), ("d", q + t, has_down, down)
        ):
            real = source >= first if way == "u" else source < nchip
            if way == "d" and first > 0:
                real = jnp.logical_and(real, source >= first)
            ref = slot(source, core)
            guard(real)(functools.partial(arrived, ref, (name, way, t), nxt))
            if t < nchip - 1:
                push(ref, ref, (name, way, t), (name, way, t + 1), nxt, both(real, more))
            push(ref, ref, (name, "m", way, t), (name, "m", way, t), mate, real)

    def chain_mate(name, t):
        first, slot, _, _ = chains[name]
        if t == 0:
            mine = None if first == 0 else q >= first
            guard(mine)(functools.partial(arrived, slot(q, 1 - core), (name, "m", 0), mate))
            return
        for way, source in (("u", q - t), ("d", q + t)):
            real = source >= first if way == "u" else source < nchip
            if way == "d" and first > 0:
                real = jnp.logical_and(real, source >= first)
            guard(real)(
                functools.partial(arrived, slot(source, 1 - core), (name, "m", way, t), mate)
            )

    def stack(buf):
        def place(origin, part, e):
            if part is None:
                return buf.at[:, origin]
            return buf.at[:, origin, pl.ds(part * (rblk // 2), rblk // 2), :]
        return place

    def dstack(m, p):
        def place(origin, part, e):
            if part is None:
                return dg.at[m, p, origin, low[p]:, e]
            return dg.at[m, p, origin, low[p]:, e, pl.ds(part * (kb // 2), kb // 2), :]
        return place

    rings = {"k": (stack(kg), False), "u": (stack(ug), False)}
    for m in range(2):
        for p in range(pc):
            rings["e", m, p] = (dstack(m, p), True)

    def ring_own(name, src=None):
        place, _ = rings[name]
        own = place(row, None, core)
        src = own if src is None else src
        push(src, own, (name, "R", 0), (name, "R", 1), right)
        push(src, own, (name, "L", 0), (name, "L", 1), left)

    def ring_hop(name, t):
        place, shared = rings[name]
        for way, sign, part, nxt in (("R", -1, 0, right), ("L", 1, 1, left)):
            origin = row_at(sign * t)
            got = None if t < half_ring else part
            ref = place(origin, got, core)
            arrived(ref, (name, way, t), nxt)
            if t < half_ring:
                fwd = place(origin, None if t + 1 < half_ring else part, core)
                push(fwd, fwd, (name, way, t), (name, way, t + 1), nxt)
            if shared:
                push(ref, ref, (name, "m", way, t), (name, "m", way, t), mate)

    def ring_mate(name):
        place, _ = rings[name]
        for t in range(1, half_ring + 1):
            for way, sign, part in (("R", -1, 0), ("L", 1, 1)):
                got = None if t < half_ring else part
                arrived(place(row_at(sign * t), got, 1 - core), (name, "m", way, t), mate)

    hops = range(1, nchip)
    rhops = range(1, half_ring + 1)
    dnames = [[("d", m, p) for p in range(pc)] for m in range(2)]
    enames = [[("e", m, p) for p in range(pc)] for m in range(2)]

    group = nb // pc
    chunk = 256

    def right_side(rhs):
        for p in range(pc):
            for r in range(nrow):
                at = (p * nrow + r) * rblk
                hi, lo = split(rhs[p, r])
                bh[at : at + rblk, :] = hi
                bl[at : at + rblk, :] = lo

    def left_side(m):
        for p in range(pc):
            for r in range(nrow):
                at = (p * nrow + r) * rblk
                hi, lo = split(dg[m, p, r, low[p]:].reshape(nb - p * group, rblk))
                dh[p * group :, at : at + rblk] = hi
                dl[p * group :, at : at + rblk] = lo

    def solve(m):
        for g in range(pc):
            rows = slice(g * group, (g + 1) * group)
            deep = (g + 1) * group
            for n in range(0, width, chunk):
                cols = slice(n, n + chunk)
                w = dot3(dh[rows, :deep], dl[rows, :deep], bh[:deep, cols], bl[:deep, cols])
                wf[m, rows, cols] = w
                hi, lo = split(w)
                wh[m, rows, cols] = hi
                wl[m, rows, cols] = lo

    outs = []

    def emit(src, dst, index):
        copy = pltpu.make_async_copy(src, dst, osem.at[index])
        copy.start()
        outs.append(copy)

    def own_rows(m):
        for p in range(pc):
            at = pl.multiple_of((p * nrow + row) * rblk, rblk)
            emit(wf.at[m, pl.ds(at, rblk), :], out_ref.at[m * pc + p], m * pc + p)

    deep = 2 * kb

    def slab(panel, begin, block, count, m, chip):
        tile = 2 if count % 2 == 0 else 1
        size = tile * rblk
        rows = pl.ds(pl.multiple_of(chip * deep, deep), deep)

        def step(i, carry):
            cols = pl.ds(pl.multiple_of(begin + i * size, rblk), size)
            th, tl = split(panel[rows, cols].T)
            part = dot3(th, tl, wh[m, rows, :], wl[m, rows, :])
            kloc[pl.ds(block + i * tile, tile)] -= part.reshape(tile, rblk, width)
            return carry

        lax.fori_loop(0, count // tile, step, 0)

    first_half, second_half = rest // 2, rest - rest // 2
    uses = {
        "f2": (fg, height, pc, rest, 0),
        "s0": (sg, 0, pc, first_half, 1),
        "s1": (sg, cut, pc + first_half, second_half, 1),
    }

    def phase(name, t):
        chain_mate(name, t)
        if t == 0:
            slab(*uses[name], q)
            return
        for source, real in ((q - t, q >= t), (q + t, q + t < nchip)):
            pl.when(real)(functools.partial(slab, *uses[name], source))

    def hop(name, t):
        if t < nchip:
            chain_hop(name, t)

    panels = ("s0", "s1")
    ring_own("k", k_ref.at[:pc])
    staged = {name: stage(name) for name in chains}
    kmine = pltpu.make_async_copy(k_ref.at[:pc], kg.at[:, row], sem("l", "k"))
    kmine.start()
    kall = pltpu.make_async_copy(k_ref.at[pc:], kloc, sem("l", "kall"))
    kall.start()
    for name in dnames[0] + ["f1"] + dnames[1]:
        chain_own(name, staged[name])
    for t in hops:
        for name in dnames[0]:
            chain_hop(name, t)
    for ring in enames[0]:
        ring_own(ring)
    for t in hops:
        for name in ["f1"] + dnames[1]:
            chain_hop(name, t)
    for name in ("f2",) + panels:
        chain_own(name, staged[name])
    for t in rhops[:-1]:
        ring_hop("k", t)
    for ring in enames[1]:
        ring_own(ring)
    for t in rhops[:-1]:
        for ring in enames[0]:
            ring_hop(ring, t)
    ring_hop("k", half_ring)
    kmine.wait()
    right_side(kg)
    for ring in enames[0]:
        ring_hop(ring, half_ring)
    for t in range(nchip):
        for name in dnames[0]:
            chain_mate(name, t)
    for ring in enames[0]:
        ring_mate(ring)
    left_side(0)
    solve(0)
    hop("f2", 1)
    for t in range(nchip):
        chain_mate("f1", t)
    kall.wait()
    th, tl = split(fg[:, :height].T)
    first = dot3(th, tl, wh[0], wl[0])
    ug[:, row] = kloc[:pc] - first.reshape(pc, rblk, width)
    ring_own("u")
    own_rows(0)
    for t in rhops[:-1]:
        for ring in enames[1]:
            ring_hop(ring, t)
    phase("f2", 0)
    for name in panels:
        hop(name, 1)
    for ring in enames[1]:
        ring_hop(ring, half_ring)
    for t in range(nchip):
        for name in dnames[1]:
            chain_mate(name, t)
    for ring in enames[1]:
        ring_mate(ring)
    left_side(1)
    phase("f2", 1)
    hop("f2", 2)
    for t in rhops[:-1]:
        ring_hop("u", t)
    if nchip > 2:
        phase("f2", 2)
    for name in panels:
        hop(name, 2)
    ring_hop("u", half_ring)
    right_side(ug)
    solve(1)
    own_rows(1)
    for t in range(min(3, nchip)):
        for name in panels:
            phase(name, t)
    for t in range(3, nchip):
        hop("f2", t)
        phase("f2", t)
        for name in panels:
            hop(name, t)
        for name in panels:
            phase(name, t)
    emit(kloc.at[pc:], out_ref.at[2 * pc :], 2 * pc)
    for cond, copy in sent:
        guard(cond)(copy.wait_send)
    for copy in outs:
        copy.wait()


def shards(stiffness, lower_first, lower_second, diag_inv):
    cycles, _, rblk, width = stiffness.shape
    nrow, ncol = lax.axis_size("row"), lax.axis_size("col")
    kb = lower_first.shape[0]
    pc = diag_inv.shape[2]
    nb = kb * ncol
    nchip = ncol // 2
    sem_count = (4 + 2 * pc) * (8 * nchip + 8) + 40 * (2 + 2 * pc) * max(1, nrow // 4)
    sem_count = 2 * sem_count + 2 * lower_first.shape[1]
    dims = (nrow, ncol, pc, rblk, kb, sem_count)
    out = pl.pallas_call(
        functools.partial(kernel, dims),
        out_shape=jax.ShapeDtypeStruct((cycles, rblk, width), F32),
        in_specs=[pl.BlockSpec(memory_space=pl.ANY)] * 4,
        out_specs=pl.BlockSpec(memory_space=pl.ANY),
        scratch_shapes=[
            pltpu.VMEM((pc, nrow, rblk, width), F32),
            pltpu.VMEM((pc, nrow, rblk, width), F32),
            pltpu.VMEM((nb, lower_first.shape[1] * rblk), F32),
            pltpu.VMEM((nb, lower_second.shape[1] * rblk), F32),
            pltpu.VMEM((2, pc, nrow, nchip, 2, kb, rblk), F32),
            pltpu.VMEM((cycles - pc, rblk, width), F32),
            pltpu.VMEM((nb, width), BF16),
            pltpu.VMEM((nb, width), BF16),
            pltpu.VMEM((nb, nb), BF16),
            pltpu.VMEM((nb, nb), BF16),
            pltpu.VMEM((2, nb, width), BF16),
            pltpu.VMEM((2, nb, width), BF16),
            pltpu.VMEM((2, nb, width), F32),
            pltpu.SemaphoreType.DMA((sem_count,)),
            pltpu.SemaphoreType.DMA((2 * pc + 1,)),
        ],
        compiler_params=pltpu.CompilerParams(
            collective_id=0, has_side_effects=True, vmem_limit_bytes=63 << 20
        ),
    )(
        stiffness.reshape(cycles, rblk, width),
        lower_first,
        lower_second,
        diag_inv,
    )
    return out.reshape(cycles, 1, rblk, width)


def solution(mesh):
    placed = (
        P(None, "row", None, "col"),
        P("col", None, "row", None),
        P("col", None, "row", None),
        P(None, "col", None, "row", None),
    )
    return jax.shard_map(
        shards, mesh=mesh, in_specs=placed, out_specs=P(None, "row", None, "col"), check_vma=False
    )
```

```python
import functools

import jax
import jax.numpy as jnp
from jax import lax
from jax.experimental import pallas as pl
from jax.experimental.pallas import tpu as pltpu
from jax.sharding import PartitionSpec as P

MESH = pl.DeviceIdType.MESH
F32 = jnp.float32
BF16 = jnp.bfloat16


def split(value):
    high = value.astype(BF16)
    return high, (value - high.astype(F32)).astype(BF16)


def dot3(ah, al, bh, bl):
    d = functools.partial(jnp.dot, preferred_element_type=F32)
    return d(ah, bh) + (d(ah, bl) + d(al, bh))


def kernel(
    dims, k_ref, f_ref, s_ref, d_ref, out_ref,
    kg, ug, fg, sg, dg, kloc, bh, bl, dh, dl, wh, wl, wf, sems, osem,
):
    nrow, ncol, pc, rblk, kb, sem_count = dims
    nchip = ncol // 2
    nb = kb * ncol
    width = k_ref.shape[2]
    cycles = k_ref.shape[0]
    height = pc * rblk
    half_ring = nrow // 2
    row, col = lax.axis_index("row"), lax.axis_index("col")
    q, core = col // 2, col % 2
    partner = col + 1 - 2 * core

    def flip(i):
        return i + (i // half_ring) * (3 * half_ring - 1 - 2 * i)

    pos = flip(row)

    def row_at(shift):
        return flip((pos + shift + nrow) % nrow)

    table = {}

    def sem(*key):
        index = table.setdefault(key, len(table))
        assert index < sem_count
        return sems.at[index]

    sent = []

    def always(fn):
        fn()

    def guard(cond):
        return always if cond is None else pl.when(cond)

    def both(a, b):
        if a is None:
            return b
        return a if b is None else jnp.logical_and(a, b)

    def push(src, dst, skey, rkey, device, cond=None):
        copy = pltpu.make_async_remote_copy(
            src_ref=src, dst_ref=dst, send_sem=sem("s", *skey), recv_sem=sem("r", *rkey),
            device_id=device, device_id_type=MESH,
        )
        guard(cond)(copy.start)
        sent.append((cond, copy))

    def arrived(dst, rkey, device):
        pltpu.make_async_remote_copy(
            src_ref=dst, dst_ref=dst, send_sem=sem("s", *rkey), recv_sem=sem("r", *rkey),
            device_id=device, device_id_type=MESH,
        ).wait_recv()

    barrier = pltpu.get_barrier_semaphore()
    right, left = {"row": row_at(1)}, {"row": row_at(-1)}
    up, down, mate = {"col": col + 2}, {"col": col - 2}, {"col": partner}
    for device in (right, left, mate):
        pl.semaphore_signal(barrier, inc=1, device_id=device, device_id_type=MESH)
    has_up, has_down = q < nchip - 1, q > 0

    @pl.when(has_up)
    def _():
        pl.semaphore_signal(barrier, inc=1, device_id=up, device_id_type=MESH)

    @pl.when(has_down)
    def _():
        pl.semaphore_signal(barrier, inc=1, device_id=down, device_id_type=MESH)

    spans = nchip - 1
    pl.semaphore_wait(barrier, 3 + (2 * spans - 1 - q) // spans + (q + spans - 1) // spans)

    def fslot(buf, lo, hi):
        return lambda chip, e: buf.at[pl.ds(pl.multiple_of((chip * 2 + e) * kb, kb), kb), lo:hi]

    def dslot(m, p):
        return lambda chip, e: dg.at[m, p, row, chip, e]

    low = [p * nchip // pc for p in range(pc)]
    rest = cycles - 2 * pc
    cut = rest // 2 * rblk
    chains = {}
    for m in range(2):
        for p in range(pc):
            chains["d", m, p] = (low[p], dslot(m, p), d_ref, None)
    chains["f1"] = (0, fslot(fg, 0, height), f_ref, (0, pc))
    chains["f2"] = (0, fslot(fg, height, height + rest * rblk), f_ref, (pc, pc + rest))
    chains["s0"] = (0, fslot(sg, 0, cut), s_ref, (0, rest // 2))
    chains["s1"] = (0, fslot(sg, cut, rest * rblk), s_ref, (rest // 2, rest))

    def stage(name):
        _, slot, src, span = chains[name]
        if span is None:
            _, m, p = name
            pieces = [(src.at[m, :, p, 0, :], slot(q, core))]
        else:
            mine = slot(q, core)
            pieces = [
                (src.at[:, j, 0, :], mine.at[:, (j - span[0]) * rblk : (j - span[0] + 1) * rblk])
                for j in range(*span)
            ]
        copies = []
        for i, (here, there) in enumerate(pieces):
            copies.append(pltpu.make_async_copy(here, there, sem("l", name, i)))
            copies[-1].start()
        return copies

    def chain_own(name, copies):
        first, slot, _, _ = chains[name]
        for copy in copies:
            copy.wait()
        mine = None if first == 0 else q >= first
        own = slot(q, core)
        push(own, own, (name, "u", 0), (name, "u", 1), up, both(mine, has_up))
        push(own, own, (name, "d", 0), (name, "d", 1), down, both(mine, has_down))
        push(own, own, (name, "m", 0), (name, "m", 0), mate, mine)

    def chain_hop(name, t):
        first, slot, _, _ = chains[name]
        for way, source, more, nxt in (
            ("u", q - t, has_up, up), ("d", q + t, has_down, down)
        ):
            real = source >= first if way == "u" else source < nchip
            if way == "d" and first > 0:
                real = jnp.logical_and(real, source >= first)
            ref = slot(source, core)
            guard(real)(functools.partial(arrived, ref, (name, way, t), nxt))
            if t < nchip - 1:
                push(ref, ref, (name, way, t), (name, way, t + 1), nxt, both(real, more))
            push(ref, ref, (name, "m", way, t), (name, "m", way, t), mate, real)

    def chain_mate(name, t):
        first, slot, _, _ = chains[name]
        if t == 0:
            mine = None if first == 0 else q >= first
            guard(mine)(functools.partial(arrived, slot(q, 1 - core), (name, "m", 0), mate))
            return
        for way, source in (("u", q - t), ("d", q + t)):
            real = source >= first if way == "u" else source < nchip
            if way == "d" and first > 0:
                real = jnp.logical_and(real, source >= first)
            guard(real)(
                functools.partial(arrived, slot(source, 1 - core), (name, "m", way, t), mate)
            )

    def stack(buf):
        def place(origin, part, e):
            if part is None:
                return buf.at[:, origin]
            return buf.at[:, origin, pl.ds(part * (rblk // 2), rblk // 2), :]
        return place

    def dstack(m, p):
        def place(origin, part, e):
            if part is None:
                return dg.at[m, p, origin, low[p]:, e]
            return dg.at[m, p, origin, low[p]:, e, pl.ds(part * (kb // 2), kb // 2), :]
        return place

    rings = {"k": (stack(kg), False), "u": (stack(ug), False)}
    for m in range(2):
        for p in range(pc):
            rings["e", m, p] = (dstack(m, p), True)

    def ring_own(name, src=None):
        place, _ = rings[name]
        own = place(row, None, core)
        src = own if src is None else src
        push(src, own, (name, "R", 0), (name, "R", 1), right)
        push(src, own, (name, "L", 0), (name, "L", 1), left)

    def ring_hop(name, t):
        place, shared = rings[name]
        for way, sign, part, nxt in (("R", -1, 0, right), ("L", 1, 1, left)):
            origin = row_at(sign * t)
            got = None if t < half_ring else part
            ref = place(origin, got, core)
            arrived(ref, (name, way, t), nxt)
            if t < half_ring:
                fwd = place(origin, None if t + 1 < half_ring else part, core)
                push(fwd, fwd, (name, way, t), (name, way, t + 1), nxt)
            if shared:
                push(ref, ref, (name, "m", way, t), (name, "m", way, t), mate)

    def ring_mate(name):
        place, _ = rings[name]
        for t in range(1, half_ring + 1):
            for way, sign, part in (("R", -1, 0), ("L", 1, 1)):
                got = None if t < half_ring else part
                arrived(place(row_at(sign * t), got, 1 - core), (name, "m", way, t), mate)

    hops = range(1, nchip)
    rhops = range(1, half_ring + 1)
    dnames = [[("d", m, p) for p in range(pc)] for m in range(2)]
    enames = [[("e", m, p) for p in range(pc)] for m in range(2)]

    group = nb // pc
    chunk = 256

    def right_side(rhs):
        for p in range(pc):
            for r in range(nrow):
                at = (p * nrow + r) * rblk
                hi, lo = split(rhs[p, r])
                bh[at : at + rblk, :] = hi
                bl[at : at + rblk, :] = lo

    def left_side(m):
        for p in range(pc):
            for r in range(nrow):
                at = (p * nrow + r) * rblk
                hi, lo = split(dg[m, p, r, low[p]:].reshape(nb - p * group, rblk))
                dh[p * group :, at : at + rblk] = hi
                dl[p * group :, at : at + rblk] = lo

    def solve(m):
        for g in range(pc):
            rows = slice(g * group, (g + 1) * group)
            deep = (g + 1) * group
            for n in range(0, width, chunk):
                cols = slice(n, n + chunk)
                w = dot3(dh[rows, :deep], dl[rows, :deep], bh[:deep, cols], bl[:deep, cols])
                wf[m, rows, cols] = w
                hi, lo = split(w)
                wh[m, rows, cols] = hi
                wl[m, rows, cols] = lo

    outs = []

    def emit(src, dst, index):
        copy = pltpu.make_async_copy(src, dst, osem.at[index])
        copy.start()
        outs.append(copy)

    def own_rows(m):
        for p in range(pc):
            at = pl.multiple_of((p * nrow + row) * rblk, rblk)
            emit(wf.at[m, pl.ds(at, rblk), :], out_ref.at[m * pc + p], m * pc + p)

    deep = 2 * kb

    def slab(panel, begin, block, count, m, chip):
        tile = 2 if count % 2 == 0 else 1
        size = tile * rblk
        rows = pl.ds(pl.multiple_of(chip * deep, deep), deep)

        def step(i, carry):
            cols = pl.ds(pl.multiple_of(begin + i * size, rblk), size)
            th, tl = split(panel[rows, cols].T)
            part = dot3(th, tl, wh[m, rows, :], wl[m, rows, :])
            kloc[pl.ds(block + i * tile, tile)] -= part.reshape(tile, rblk, width)
            return carry

        lax.fori_loop(0, count // tile, step, 0)

    first_half, second_half = rest // 2, rest - rest // 2
    uses = {
        "f2": (fg, height, pc, rest, 0),
        "s0": (sg, 0, pc, first_half, 1),
        "s1": (sg, cut, pc + first_half, second_half, 1),
    }

    def phase(name, t):
        chain_mate(name, t)
        if t == 0:
            slab(*uses[name], q)
            return
        for source, real in ((q - t, q >= t), (q + t, q + t < nchip)):
            pl.when(real)(functools.partial(slab, *uses[name], source))

    def hop(name, t):
        if t < nchip:
            chain_hop(name, t)

    panels = ("s0", "s1")
    ring_own("k", k_ref.at[:pc])
    staged = {name: stage(name) for name in chains}
    kmine = pltpu.make_async_copy(k_ref.at[:pc], kg.at[:, row], sem("l", "k"))
    kmine.start()
    kall = pltpu.make_async_copy(k_ref.at[pc:], kloc, sem("l", "kall"))
    kall.start()
    for name in dnames[0] + ["f1"] + dnames[1]:
        chain_own(name, staged[name])
    for t in hops:
        for name in dnames[0]:
            chain_hop(name, t)
    for ring in enames[0]:
        ring_own(ring)
    early = ["f1"] + dnames[1]
    for name in early:
        chain_hop(name, 1)
    chain_own("f2", staged["f2"])
    for t in hops[1:]:
        for name in early:
            chain_hop(name, t)
    for name in panels:
        chain_own(name, staged[name])
    for t in rhops[:-1]:
        ring_hop("k", t)
    for t in rhops[:-1]:
        for ring in enames[0]:
            ring_hop(ring, t)
    for ring in enames[1]:
        ring_own(ring)
    ring_hop("k", half_ring)
    kmine.wait()
    right_side(kg)
    hop("f2", 1)
    for ring in enames[0]:
        ring_hop(ring, half_ring)
    for t in range(nchip):
        for name in dnames[0]:
            chain_mate(name, t)
    for ring in enames[0]:
        ring_mate(ring)
    left_side(0)
    solve(0)
    for t in range(nchip):
        chain_mate("f1", t)
    kall.wait()
    th, tl = split(fg[:, :height].T)
    first = dot3(th, tl, wh[0], wl[0])
    ug[:, row] = kloc[:pc] - first.reshape(pc, rblk, width)
    ring_own("u")
    for t in rhops[:-1]:
        for ring in enames[1]:
            ring_hop(ring, t)
    for name in panels:
        hop(name, 1)
    own_rows(0)
    phase("f2", 0)
    for ring in enames[1]:
        ring_hop(ring, half_ring)
    for t in range(nchip):
        for name in dnames[1]:
            chain_mate(name, t)
    for ring in enames[1]:
        ring_mate(ring)
    hop("f2", 2)
    left_side(1)
    phase("f2", 1)
    for name in panels:
        hop(name, 2)
    for t in rhops[:-1]:
        ring_hop("u", t)
    if nchip > 2:
        phase("f2", 2)
    ring_hop("u", half_ring)
    right_side(ug)
    solve(1)
    own_rows(1)
    for t in range(min(3, nchip)):
        for name in panels:
            phase(name, t)
    for t in range(3, nchip):
        hop("f2", t)
        phase("f2", t)
        for name in panels:
            hop(name, t)
        for name in panels:
            phase(name, t)
    emit(kloc.at[pc:], out_ref.at[2 * pc :], 2 * pc)
    for cond, copy in sent:
        guard(cond)(copy.wait_send)
    for copy in outs:
        copy.wait()


def shards(stiffness, lower_first, lower_second, diag_inv):
    cycles, _, rblk, width = stiffness.shape
    nrow, ncol = lax.axis_size("row"), lax.axis_size("col")
    kb = lower_first.shape[0]
    pc = diag_inv.shape[2]
    nb = kb * ncol
    nchip = ncol // 2
    sem_count = (4 + 2 * pc) * (8 * nchip + 8) + 40 * (2 + 2 * pc) * max(1, nrow // 4)
    sem_count = 2 * sem_count + 2 * lower_first.shape[1]
    dims = (nrow, ncol, pc, rblk, kb, sem_count)
    out = pl.pallas_call(
        functools.partial(kernel, dims),
        out_shape=jax.ShapeDtypeStruct((cycles, rblk, width), F32),
        in_specs=[pl.BlockSpec(memory_space=pl.ANY)] * 4,
        out_specs=pl.BlockSpec(memory_space=pl.ANY),
        scratch_shapes=[
            pltpu.VMEM((pc, nrow, rblk, width), F32),
            pltpu.VMEM((pc, nrow, rblk, width), F32),
            pltpu.VMEM((nb, lower_first.shape[1] * rblk), F32),
            pltpu.VMEM((nb, lower_second.shape[1] * rblk), F32),
            pltpu.VMEM((2, pc, nrow, nchip, 2, kb, rblk), F32),
            pltpu.VMEM((cycles - pc, rblk, width), F32),
            pltpu.VMEM((nb, width), BF16),
            pltpu.VMEM((nb, width), BF16),
            pltpu.VMEM((nb, nb), BF16),
            pltpu.VMEM((nb, nb), BF16),
            pltpu.VMEM((2, nb, width), BF16),
            pltpu.VMEM((2, nb, width), BF16),
            pltpu.VMEM((2, nb, width), F32),
            pltpu.SemaphoreType.DMA((sem_count,)),
            pltpu.SemaphoreType.DMA((2 * pc + 1,)),
        ],
        compiler_params=pltpu.CompilerParams(
            collective_id=0, has_side_effects=True, vmem_limit_bytes=63 << 20
        ),
    )(
        stiffness.reshape(cycles, rblk, width),
        lower_first,
        lower_second,
        diag_inv,
    )
    return out.reshape(cycles, 1, rblk, width)


def solution(mesh):
    placed = (
        P(None, "row", None, "col"),
        P("col", None, "row", None),
        P("col", None, "row", None),
        P(None, "col", None, "row", None),
    )
    return jax.shard_map(
        shards, mesh=mesh, in_specs=placed, out_specs=P(None, "row", None, "col"), check_vma=False
    )
```
